768 devices in a mesh: ctx: 24 (over z, x_hi), tp: 32 (over x_lo, y, core).
Axes of the slice: x: 4 (x_hi: 2, x_lo: 2; x = x_hi * 2 + x_lo), y: 8, z: 12, core: 2. Of those that a mesh axis runs over, the one named last changes fastest.
Arguments:
- tokens: bfloat16 [6144, 4096], P('ctx', 'tp'), may hold values from -6 to 6
- cotangent: bfloat16 [6144, 4096], P('ctx', 'tp'), may hold values from -6 to 6
- in_weight: bfloat16 [4096, 3, 4096], P(None, None, 'tp'), may hold values from -0.09375 to 0.09375
- filter_taps: float32 [128, 4096], P(None, 'tp'), may hold values from -0.5 to 0.5
- out_weight: bfloat16 [4096, 4096], P('tp'), may hold values from -0.09375 to 0.09375
- segment_ids: int32 [6144], replicated, may hold values from 0 to 47, never falling along the last dimension, each value on 1 to 512 neighbouring positions
Outputs:
- block_out: bfloat16 [6144, 4096], P('ctx', 'tp')
- input_grad: bfloat16 [6144, 4096], P('ctx', 'tp')
The draws below stay inside these ranges and needn't reach their ends.
Inputs may be any that keep to these rules, and one draw needn't show every extreme that they name: `segment_ids`: never falls along the sequence; every number 0 to 47 names one contig of 1 to 512 positions, and at least one contig has exactly 512.
All inputs are finite; a program needn't handle non-finite values.
Results may differ from the reference program's by a relative error of at most 0.024.
Values may be sent and summed in bfloat16 or wider, within the bound.
No kernel may reach another device: no remote copies, remote signals or barrier semaphores. Data moves between devices by JAX's collectives and lax.ppermute only.
A program may use at most 32 MiB of HBM per device.

```python
import math
import jax
import jax.numpy as jnp
import numpy as np
from jax import lax

D = 4096
FILT = 128
TOKENS = 6144
SEGS = 48
SEG_MOST = 512
N_TP = 32


def levels(own_key, dims, shards, smallest, high):
    level = 1.0
    for axis_at, shards_of in shards:
        steps = jax.random.uniform(jax.random.fold_in(jax.random.fold_in(own_key, 6), axis_at), (shards_of,), jnp.float32, smallest / len(shards), high / len(shards))
        level = level * jnp.repeat(jnp.exp(steps), dims[axis_at] // shards_of).reshape((-1,) + (1,) * (len(dims) - 1 - axis_at))
    return level


def profile(number_of, total, limit, lean):
    weights = [(1 << 20) // math.isqrt(standing ** lean) + 1 for standing in range(2, number_of + 1)]
    rest, holding = total - limit - (number_of - 1), [1] * (number_of - 1)
    while rest > 0:
        free = [i for i in range(number_of - 1) if holding[i] < limit]
        whole, budget = sum([weights[i] for i in free]), rest
        for i in free:
            addition = min(limit - holding[i], max(1, budget * weights[i] // whole), rest)
            holding[i] = holding[i] + addition
            rest = rest - addition
    return np.array([limit] + holding)


def uneven(key, count, total, most, lean):
    if count == 2:
        one = jax.random.randint(key, (), max(1, total - most), min(most, total - 1) + 1)
        return jnp.stack([one, total - one])
    tallies = jnp.asarray(profile(count, total, most, lean), jnp.int32)
    pairs = (count - 1) // 2
    source_of, sink = tallies[1:1 + 2 * pairs:2], tallies[2:2 + 2 * pairs:2]
    margin = jnp.minimum(source_of - 1, most - sink)
    moved = jax.random.randint(jax.random.fold_in(key, 1), (pairs,), 0, 1 << 20) % (margin + 1)
    tallies = tallies.at[1:1 + 2 * pairs:2].set(source_of - moved).at[2:2 + 2 * pairs:2].set(sink + moved)
    return tallies[jax.random.permutation(jax.random.fold_in(key, 2), count)]


def centred(stream_key, extent, spread, most, pieces=(), kind=jnp.bfloat16):
    drawn = spread * jax.random.normal(stream_key, extent, jnp.float32)
    if pieces:
        drawn = drawn * levels(stream_key, extent, pieces, -0.22, 0.18)
    return jnp.clip(drawn, -most, most).astype(kind)


def setup_inputs(seed: int = 0) -> dict:
    splits = jax.random.split(jax.random.key(seed), 7)
    tokens = centred(splits[0], (TOKENS, D), 1.0, 6.0, ((0, 24), (1, 32)))
    cotangent = centred(splits[1], (TOKENS, D), 1.0, 6.0, ((0, 24), (1, 32)))
    in_weight = centred(splits[2], (D, 3, D), D ** -0.5, 0.09375, ((2, 32),))
    filter_taps = centred(splits[3], (FILT, D), FILT ** -0.5, 0.5, ((1, 32),), jnp.float32)
    out_weight = centred(splits[4], (D, D), D ** -0.5, 0.09375, ((0, 32),))
    segment_ids = jnp.searchsorted(jnp.cumsum(uneven(splits[5], SEGS, TOKENS, SEG_MOST, 2)), jnp.arange(TOKENS), side="right").astype(jnp.int32)
    return {"tokens": tokens, "cotangent": cotangent, "in_weight": in_weight, "filter_taps": filter_taps, "out_weight": out_weight, "segment_ids": segment_ids}


def reach_of(segment_ids):
    pos = jnp.arange(TOKENS, dtype=jnp.int32)
    change = jnp.concatenate([jnp.ones((1,), bool), segment_ids[1:] != segment_ids[:-1]])
    starts = jnp.where(change, pos, jnp.zeros_like(pos))
    return pos - lax.cummax(starts, axis=0)


def reference(tokens, cotangent, in_weight, filter_taps, out_weight, segment_ids):
    chans = D // N_TP
    proj = jnp.dot(tokens, in_weight.reshape(D, 3 * D), preferred_element_type=jnp.float32).astype(jnp.bfloat16)
    proj = proj.reshape(TOKENS, 3, D)
    q = proj[:, 0].astype(jnp.float32)
    k = proj[:, 1].astype(jnp.float32)
    v = proj[:, 2].astype(jnp.float32)
    mix = (k * v).astype(jnp.bfloat16).astype(jnp.float32)
    reach = reach_of(segment_ids)
    padded = jnp.concatenate([jnp.zeros((FILT, D), jnp.float32), mix], 0)

    def fwd_tap(s, acc):
        s = s.astype(jnp.int32)
        piece = lax.dynamic_slice_in_dim(padded, FILT - s, TOKENS, 0)
        tap = lax.dynamic_index_in_dim(filter_taps, s, 0, keepdims=False)
        return acc + tap[None, :] * piece * (s <= reach)[:, None].astype(jnp.float32)

    conv = lax.fori_loop(0, FILT, fwd_tap, jnp.zeros((TOKENS, D), jnp.float32))
    gated = (q * conv).astype(jnp.bfloat16)

    def out_group(j, acc):
        j = j.astype(jnp.int32)
        left = lax.dynamic_slice_in_dim(gated, j * chans, chans, 1)
        right = lax.dynamic_slice_in_dim(out_weight, j * chans, chans, 0)
        term = jnp.dot(left, right, preferred_element_type=jnp.float32).astype(jnp.bfloat16)
        return acc + term.astype(jnp.float32)

    block_out = lax.fori_loop(0, N_TP, out_group, jnp.zeros((TOKENS, D), jnp.float32)).astype(jnp.bfloat16)
    dgated = jnp.dot(cotangent, out_weight.T, preferred_element_type=jnp.float32)
    dq = dgated * conv
    dconv = (dgated * q).astype(jnp.bfloat16).astype(jnp.float32)
    padded_d = jnp.concatenate([dconv, jnp.zeros((FILT, D), jnp.float32)], 0)
    padded_r = jnp.concatenate([reach, jnp.zeros((FILT,), jnp.int32)], 0)

    def bwd_tap(s, acc):
        s = s.astype(jnp.int32)
        piece = lax.dynamic_slice_in_dim(padded_d, s, TOKENS, 0)
        rpiece = lax.dynamic_slice_in_dim(padded_r, s, TOKENS, 0)
        tap = lax.dynamic_index_in_dim(filter_taps, s, 0, keepdims=False)
        return acc + tap[None, :] * piece * (s <= rpiece)[:, None].astype(jnp.float32)

    dmix = lax.fori_loop(0, FILT, bwd_tap, jnp.zeros((TOKENS, D), jnp.float32))
    dproj = jnp.stack([dq, dmix * v, dmix * k], axis=1).astype(jnp.bfloat16)

    def grad_group(j, acc):
        j = j.astype(jnp.int32)
        left = lax.dynamic_slice_in_dim(dproj, j * chans, chans, 2).reshape(TOKENS, 3 * chans)
        right = lax.dynamic_slice_in_dim(in_weight, j * chans, chans, 2).reshape(D, 3 * chans)
        term = jnp.dot(left, right.T, preferred_element_type=jnp.float32).astype(jnp.bfloat16)
        return acc + term.astype(jnp.float32)

    input_grad = lax.fori_loop(0, N_TP, grad_group, jnp.zeros((TOKENS, D), jnp.float32)).astype(jnp.bfloat16)
    return block_out, input_grad
```

```python
import jax
import jax.numpy as jnp
from jax import lax
from jax.experimental import pallas as pl
from jax.experimental.pallas import tpu as pltpu
from jax.sharding import Mesh
from jax.sharding import PartitionSpec as P

X, Y, CORE = 2, 8, 2
SWAP = [(0, 1), (1, 0)]
LANES = 128
STRIP = 64
INTERPRET = False
BF, F32 = jnp.bfloat16, jnp.float32


def f32(a):
    return a.astype(F32)


def call(kernel, name, outs, scratch, flops, nbytes, *args):
    return pl.pallas_call(
        kernel,
        out_shape=[jax.ShapeDtypeStruct(s, d) for s, d in outs],
        in_specs=[pl.BlockSpec(memory_space=pltpu.SMEM)]
        + [pl.BlockSpec(memory_space=pltpu.VMEM)] * (len(args) - 1),
        out_specs=[pl.BlockSpec(memory_space=pltpu.VMEM)] * len(outs),
        scratch_shapes=scratch,
        cost_estimate=pl.CostEstimate(flops=flops, bytes_accessed=nbytes, transcendentals=0),
        compiler_params=pltpu.CompilerParams(vmem_limit_bytes=48 << 20),
        name=name,
        interpret=INTERPRET,
    )(*args)


def offset(pos, far, other, j):
    x = 1 - pos[0] if far else pos[0]
    core = 1 - pos[1] if other else pos[1]
    return pl.multiple_of(((x * Y + j) * CORE + core) * LANES, LANES)


def lay_out(pos, parts, whole):
    for at, part in enumerate(parts):
        for j in range(Y):
            whole[:, pl.ds(offset(pos, at // 2, at % 2, j), LANES)] = part[j]


def project(pos, t0, t1, t2, t3, w, q, k, v, mix, tail, whole):
    lay_out(pos, (t0, t1, t2, t3), whole)
    rhs = jnp.concatenate([w[0], w[1], w[2]], axis=1)
    proj = jnp.dot(whole[...], rhs, preferred_element_type=F32).astype(BF)
    q[...] = proj[:, :LANES]
    k[...] = proj[:, LANES : 2 * LANES]
    v[...] = proj[:, 2 * LANES :]
    product = (f32(proj[:, LANES : 2 * LANES]) * f32(proj[:, 2 * LANES :])).astype(BF)
    mix[...] = product
    tail[...] = product[-tail.shape[0] :]


def convolve(ext, limit, taps, shifted, back, result):
    total = ext.shape[0]
    for b in range(8):
        by = (total - b) % total if back else b
        shifted[b] = pltpu.roll(ext, by, 0) if by else ext
    n_taps = taps.shape[0]

    def strip(i, carry):
        at = pl.multiple_of(i * STRIP, STRIP)
        lim = limit[pl.ds(at, STRIP), :]

        def eight(a, acc):
            if back:
                start = pl.multiple_of(at + 8 * a, 8)
            else:
                start = pl.multiple_of(at + n_taps - 8 * a, 8)
            for b in range(8):
                s = 8 * a + b
                piece = shifted[b, pl.ds(start, STRIP), :]
                acc = acc + jnp.where(lim >= s, piece, 0.0) * taps[pl.ds(s, 1), :]
            return acc

        acc = lax.fori_loop(0, n_taps // 8, eight, jnp.zeros((STRIP, LANES), F32))
        result[pl.ds(at, STRIP), :] = acc
        return carry

    lax.fori_loop(0, limit.shape[0] // STRIP, strip, 0)


def forward(pos, prior, mix, q, reach, taps, w, conv, o0, o1, o2, o3, shifted):
    ext = jnp.concatenate([f32(prior[...]), f32(mix[...])], axis=0)
    convolve(ext, reach, taps, shifted, False, conv)
    gated = (f32(q[...]) * conv[...]).astype(BF)
    for far in range(2):
        own, other = (o0, o1) if far == 0 else (o2, o3)
        for j in range(Y):
            rhs = jnp.concatenate(
                [w[:, pl.ds(offset(pos, far, o, j), LANES)] for o in range(2)], axis=1
            )
            term = jnp.dot(gated, rhs, preferred_element_type=F32).astype(BF)
            own[j] = term[:, :LANES]
            other[j] = term[:, LANES:]


def back_gate(pos, c0, c1, c2, c3, w, q, conv, dq, dconv, head, whole):
    lay_out(pos, (c0, c1, c2, c3), whole)
    dgated = lax.dot_general(
        whole[...], w[...], (((1,), (1,)), ((), ())), preferred_element_type=F32
    )
    dq[...] = (dgated * conv[...]).astype(BF)
    d = (dgated * f32(q[...])).astype(BF)
    dconv[...] = d
    head[...] = d[: head.shape[0]]


def back_project(pos, dconv, after, k, v, dq, rem, taps, w, g0, g1, g2, g3, shifted, dmix):
    ext = jnp.concatenate([f32(dconv[...]), f32(after[...])], axis=0)
    convolve(ext, rem, taps, shifted, True, dmix)
    dk = (dmix[...] * f32(v[...])).astype(BF)
    dv = (dmix[...] * f32(k[...])).astype(BF)
    dproj = jnp.concatenate([dq[...], dk, dv], axis=1)
    for far in range(2):
        own, other = (g0, g1) if far == 0 else (g2, g3)
        for j in range(Y):
            rhs = jnp.concatenate(
                [
                    jnp.concatenate(
                        [w[b, pl.ds(offset(pos, far, o, j), LANES), :] for b in range(3)], axis=1
                    )
                    for o in range(2)
                ],
                axis=0,
            )
            term = lax.dot_general(
                dproj, rhs, (((1,), (1,)), ((), ())), preferred_element_type=F32
            ).astype(BF)
            own[j] = term[:, :LANES]
            other[j] = term[:, LANES:]


def passed_along(block, distance):
    devices = range(lax.axis_size("ctx"))
    route = [(i - distance, i) for i in devices if i - distance in devices]
    return lax.ppermute(block, "ctx", route)


def spread_y(block):
    copies = jnp.broadcast_to(block[None], (Y,) + block.shape)
    return lax.all_to_all(copies, "y", split_axis=0, concat_axis=0, tiled=True)


def quarters(own):
    far = lax.ppermute(own, "x", SWAP)
    return own, lax.ppermute(own, "core", SWAP), far, lax.ppermute(far, "core", SWAP)


def summed(own_own, own_other, far_own, far_other):
    got = lax.ppermute(far_other, "core", SWAP)
    sent = (f32(far_own) + f32(got)).astype(BF)
    near = lax.ppermute(own_other, "core", SWAP)
    got = lax.ppermute(sent, "x", SWAP)
    half = (f32(own_own) + f32(near) + f32(got)).astype(BF)
    arrived = lax.all_to_all(half, "y", split_axis=0, concat_axis=0, tiled=True)
    return f32(arrived).sum(axis=0).astype(BF)


def shards(tokens, cotangent, in_weight, filter_taps, out_weight, segment_ids):
    width, _, chans = in_weight.shape
    rows = tokens.shape[0]
    taps = filter_taps.shape[0]
    w3 = in_weight.transpose(1, 0, 2)
    pos = jnp.stack([lax.axis_index("x"), lax.axis_index("core")]).astype(jnp.int32)
    t_quarters = quarters(spread_y(tokens))
    c_quarters = quarters(spread_y(cotangent))

    base = lax.axis_index("ctx") * rows
    positions = base + jnp.arange(rows, dtype=jnp.int32)
    seg_here = lax.dynamic_slice_in_dim(segment_ids, base, rows)
    first = jnp.sum((segment_ids[None, :] < seg_here[:, None]).astype(jnp.int32), axis=1)
    end = jnp.sum((segment_ids[None, :] <= seg_here[:, None]).astype(jnp.int32), axis=1)
    reach = jnp.broadcast_to((positions - first)[:, None], (rows, chans))
    rem = jnp.broadcast_to((end - 1 - positions)[:, None], (rows, chans))

    block, edge, quarter = (rows, chans), (taps, chans), (Y, rows, LANES)
    whole = [pltpu.VMEM((rows, width), BF)]
    shifted = [pltpu.VMEM((8, rows + taps, chans), F32)]
    macs = rows * width * chans
    small = rows * width * 2
    q, k, v, mix, tail = call(
        project, "project", [(block, BF)] * 4 + [(edge, BF)], whole,
        6 * macs, small + width * chans * 6, pos, *t_quarters, w3,
    )
    prior = passed_along(tail, 1)
    conv, *terms = call(
        forward, "forward", [(block, F32)] + [(quarter, BF)] * 4, shifted,
        2 * macs, 4 * small, pos, prior, mix, q, reach, filter_taps, out_weight,
    )
    block_out = summed(*terms)
    dq, dconv, head = call(
        back_gate, "back_gate", [(block, BF)] * 2 + [(edge, BF)], whole,
        2 * macs, small + width * chans * 2, pos, *c_quarters, out_weight, q, conv,
    )
    after = passed_along(head, -1)
    terms = call(
        back_project, "back_project", [(quarter, BF)] * 4,
        shifted + [pltpu.VMEM(block, F32)],
        6 * macs, 4 * small, pos, dconv, after, k, v, dq, rem, filter_taps, w3,
    )
    return block_out, summed(*terms)


def solution(mesh):
    fine = Mesh(
        mesh.devices.reshape(mesh.shape["ctx"], X, Y, CORE), ("ctx", "x", "y", "core")
    )
    tp = ("x", "y", "core")
    placed = (P("ctx", tp), P("ctx", tp), P(None, None, tp), P(None, tp), P(tp, None), P())
    return jax.shard_map(
        shards,
        mesh=fine,
        in_specs=placed,
        out_specs=(P("ctx", tp), P("ctx", tp)),
        check_vma=False,
    )
```

```python
import jax
import jax.numpy as jnp
from jax import lax
from jax.experimental import pallas as pl
from jax.experimental.pallas import tpu as pltpu
from jax.sharding import Mesh
from jax.sharding import PartitionSpec as P

X, Y, CORE = 2, 8, 2
SWAP = [(0, 1), (1, 0)]
LANES = 128
STRIP = 64
INTERPRET = False
BF, F32 = jnp.bfloat16, jnp.float32


def f32(a):
    return a.astype(F32)


def call(kernel, outs, scratch, flops, nbytes, *args):
    return pl.pallas_call(
        kernel,
        out_shape=[jax.ShapeDtypeStruct(s, d) for s, d in outs],
        in_specs=[pl.BlockSpec(memory_space=pltpu.SMEM)]
        + [pl.BlockSpec(memory_space=pltpu.VMEM)] * (len(args) - 1),
        out_specs=[pl.BlockSpec(memory_space=pltpu.VMEM)] * len(outs),
        scratch_shapes=scratch,
        cost_estimate=pl.CostEstimate(flops=flops, bytes_accessed=nbytes, transcendentals=0),
        compiler_params=pltpu.CompilerParams(vmem_limit_bytes=48 << 20),
        interpret=INTERPRET,
    )(*args)


def offset(pos, far, other, j):
    x = 1 - pos[0] if far else pos[0]
    core = 1 - pos[1] if other else pos[1]
    return pl.multiple_of(((x * Y + j) * CORE + core) * LANES, LANES)


def lay_out(pos, parts, whole):
    for at, part in enumerate(parts):
        for j in range(Y):
            whole[:, pl.ds(offset(pos, at // 2, at % 2, j), LANES)] = part[j]


def project(pos, t0, t1, t2, t3, w, q, k, v, mix, tail, whole):
    lay_out(pos, (t0, t1, t2, t3), whole)
    rhs = jnp.concatenate([w[0], w[1], w[2]], axis=1)
    proj = jnp.dot(whole[...], rhs, preferred_element_type=F32).astype(BF)
    q[...] = proj[:, :LANES]
    k[...] = proj[:, LANES : 2 * LANES]
    v[...] = proj[:, 2 * LANES :]
    product = (f32(proj[:, LANES : 2 * LANES]) * f32(proj[:, 2 * LANES :])).astype(BF)
    mix[...] = product
    tail[...] = product[-tail.shape[0] :]


def convolve(ext, limit, taps, shifted, back, result):
    total = ext.shape[0]
    for b in range(8):
        by = (total - b) % total if back else b
        shifted[b] = pltpu.roll(ext, by, 0) if by else ext
    n_taps = taps.shape[0]

    def strip(i, carry):
        at = pl.multiple_of(i * STRIP, STRIP)
        lim = limit[pl.ds(at, STRIP), :]

        def eight(a, acc):
            if back:
                start = pl.multiple_of(at + 8 * a, 8)
            else:
                start = pl.multiple_of(at + n_taps - 8 * a, 8)
            for b in range(8):
                s = 8 * a + b
                piece = shifted[b, pl.ds(start, STRIP), :]
                acc = acc + jnp.where(lim >= s, piece, 0.0) * taps[pl.ds(s, 1), :]
            return acc

        acc = lax.fori_loop(0, n_taps // 8, eight, jnp.zeros((STRIP, LANES), F32))
        result[pl.ds(at, STRIP), :] = acc
        return carry

    lax.fori_loop(0, limit.shape[0] // STRIP, strip, 0)


def pack(pos, w, ow, sent):
    for far in range(2):
        for j in range(Y):
            off = offset(pos, far, 1, j)
            at = far * Y + j
            for b in range(3):
                sent[b, at] = w[b, pl.ds(off, LANES), :]
            sent[3, at] = ow[:, pl.ds(off, LANES)]


def filtered(pos, prior, mix, q, reach, taps, conv, gated, shifted):
    ext = jnp.concatenate([f32(prior[...]), f32(mix[...])], axis=0)
    convolve(ext, reach, taps, shifted, False, conv)
    gated[...] = (f32(q[...]) * conv[...]).astype(BF)


def slot(pos, far, j):
    return (1 - pos[0] if far else pos[0]) * Y + j


def out_terms(pos, mine, theirs, w, given, terms):
    both = jnp.concatenate([mine[...], theirs[...]], axis=1)
    for far in range(2):
        for j in range(0, Y, 2):
            rhs = jnp.concatenate(
                [
                    jnp.concatenate(
                        [w[:, pl.ds(offset(pos, far, 0, i), LANES)], given[3, far * Y + i]], axis=0
                    )
                    for i in (j, j + 1)
                ],
                axis=1,
            )
            term = jnp.dot(both, rhs, preferred_element_type=F32).astype(BF)
            terms[slot(pos, far, j)] = term[:, :LANES]
            terms[slot(pos, far, j + 1)] = term[:, LANES:]


def back_gate(pos, c0, c1, w, q, conv, dq, dconv, head, whole):
    rows = whole.shape[0]
    for other, part in enumerate((c0, c1)):
        for far in range(2):
            for j in range(Y):
                off = offset(pos, far, other, j)
                whole[:, pl.ds(off, LANES)] = part[j, far * rows : (far + 1) * rows]
    dgated = lax.dot_general(
        whole[...], w[...], (((1,), (1,)), ((), ())), preferred_element_type=F32
    )
    dq[...] = (dgated * conv[...]).astype(BF)
    d = (dgated * f32(q[...])).astype(BF)
    dconv[...] = d
    head[...] = d[: head.shape[0]]


def back_filtered(pos, dconv, after, k, v, dq, rem, taps, dproj, shifted, dmix):
    ext = jnp.concatenate([f32(dconv[...]), f32(after[...])], axis=0)
    convolve(ext, rem, taps, shifted, True, dmix)
    dproj[:, :LANES] = dq[...]
    dproj[:, LANES : 2 * LANES] = (dmix[...] * f32(v[...])).astype(BF)
    dproj[:, 2 * LANES :] = (dmix[...] * f32(k[...])).astype(BF)


def grad_terms(pos, mine, theirs, w, given, terms):
    both = jnp.concatenate([mine[...], theirs[...]], axis=1)
    for far in range(2):
        for j in range(0, Y, 2):
            rhs = jnp.concatenate(
                [
                    jnp.concatenate(
                        [w[b, pl.ds(offset(pos, far, 0, i), LANES), :] for b in range(3)]
                        + [given[b, far * Y + i] for b in range(3)],
                        axis=1,
                    )
                    for i in (j, j + 1)
                ],
                axis=0,
            )
            term = lax.dot_general(
                both, rhs, (((1,), (1,)), ((), ())), preferred_element_type=F32
            ).astype(BF)
            terms[slot(pos, far, j)] = term[:, :LANES]
            terms[slot(pos, far, j + 1)] = term[:, LANES:]


def passed_along(block, distance):
    devices = range(lax.axis_size("ctx"))
    route = [(i - distance, i) for i in devices if i - distance in devices]
    return lax.ppermute(block, "ctx", route)


def spread_y(block):
    copies = jnp.broadcast_to(block[None], (Y,) + block.shape)
    return lax.all_to_all(copies, "y", split_axis=0, concat_axis=0, tiled=True)


def swapped(block, axis):
    return lax.ppermute(block, axis, SWAP)


def summed(terms):
    arrived = lax.all_to_all(terms, ("x", "y"), split_axis=0, concat_axis=0, tiled=True)
    return f32(arrived).sum(axis=0).astype(BF)


def block_step(tokens, cotangent, in_weight, filter_taps, out_weight, segment_ids):
    width, _, chans = in_weight.shape
    rows = tokens.shape[0]
    taps = filter_taps.shape[0]
    n_chips = X * Y
    block, edge = (rows, chans), (taps, chans)
    whole = [pltpu.VMEM((rows, width), BF)]
    shifted = [pltpu.VMEM((8, rows + taps, chans), F32)]
    macs = rows * width * chans
    small = rows * width * 2

    w3 = in_weight.transpose(1, 0, 2)
    pos = jnp.stack([lax.axis_index("x"), lax.axis_index("core")]).astype(jnp.int32)
    far_cot = swapped(cotangent, "x")
    t0 = spread_y(tokens)
    (sent,) = call(pack, [((4, n_chips, LANES, chans), BF)], [], 0, 4 * small, pos, w3, out_weight)
    given = swapped(sent, "core")
    base = lax.axis_index("ctx") * rows
    positions = base + jnp.arange(rows, dtype=jnp.int32)
    seg_here = lax.dynamic_slice_in_dim(segment_ids, base, rows)
    first = jnp.sum((segment_ids[None, :] < seg_here[:, None]).astype(jnp.int32), axis=1)
    end = jnp.sum((segment_ids[None, :] <= seg_here[:, None]).astype(jnp.int32), axis=1)
    reach = jnp.broadcast_to((positions - first)[:, None], block)
    rem = jnp.broadcast_to((end - 1 - positions)[:, None], block)

    t2 = swapped(t0, "x")
    t1 = swapped(t0, "core")
    t3 = swapped(t2, "core")
    c0 = spread_y(jnp.concatenate([cotangent, far_cot], axis=0))
    c1 = swapped(c0, "core")

    q, k, v, mix, tail = call(
        project, [(block, BF)] * 4 + [(edge, BF)], whole,
        6 * macs, small + width * chans * 6, pos, t0, t1, t2, t3, w3,
    )
    prior = passed_along(tail, 1)
    conv, gated = call(
        filtered, [(block, F32), (block, BF)], shifted,
        macs, small, pos, prior, mix, q, reach, filter_taps,
    )
    theirs = swapped(gated, "core")
    (terms,) = call(
        out_terms, [((n_chips, rows, LANES), BF)], [],
        2 * macs, 2 * small, pos, gated, theirs, out_weight, given,
    )
    block_out = summed(terms)
    dq, dconv, head = call(
        back_gate, [(block, BF)] * 2 + [(edge, BF)], whole,
        2 * macs, small + width * chans * 2, pos, c0, c1, out_weight, q, conv,
    )
    after = passed_along(head, -1)
    (dproj,) = call(
        back_filtered, [((rows, 3 * chans), BF)], shifted + [pltpu.VMEM(block, F32)],
        macs, small, pos, dconv, after, k, v, dq, rem, filter_taps,
    )
    theirs = swapped(dproj, "core")
    (terms,) = call(
        grad_terms, [((n_chips, rows, LANES), BF)], [],
        6 * macs, 4 * small, pos, dproj, theirs, w3, given,
    )
    return block_out, summed(terms)


def solution(mesh):
    fine = Mesh(
        mesh.devices.reshape(mesh.shape["ctx"], X, Y, CORE), ("ctx", "x", "y", "core")
    )
    tp = ("x", "y", "core")
    placed = (P("ctx", tp), P("ctx", tp), P(None, None, tp), P(None, tp), P(tp, None), P())
    return jax.shard_map(
        block_step,
        mesh=fine,
        in_specs=placed,
        out_specs=(P("ctx", tp), P("ctx", tp)),
        check_vma=False,
    )
```

```python
import jax
import jax.numpy as jnp
from jax import lax
from jax.experimental import pallas as pl
from jax.experimental.pallas import tpu as pltpu
from jax.sharding import Mesh
from jax.sharding import PartitionSpec as P

X, Y, CORE = 2, 8, 2
SWAP = [(0, 1), (1, 0)]
LANES = 128
STRIP = 64
INTERPRET = False
BF, F32 = jnp.bfloat16, jnp.float32


def f32(a):
    return a.astype(F32)


def call(kernel, outs, scratch, flops, nbytes, *args):
    return pl.pallas_call(
        kernel,
        out_shape=[jax.ShapeDtypeStruct(s, d) for s, d in outs],
        in_specs=[pl.BlockSpec(memory_space=pltpu.SMEM)]
        + [pl.BlockSpec(memory_space=pltpu.VMEM)] * (len(args) - 1),
        out_specs=[pl.BlockSpec(memory_space=pltpu.VMEM)] * len(outs),
        scratch_shapes=scratch,
        cost_estimate=pl.CostEstimate(flops=flops, bytes_accessed=nbytes, transcendentals=0),
        compiler_params=pltpu.CompilerParams(vmem_limit_bytes=48 << 20),
        interpret=INTERPRET,
    )(*args)


def offset(pos, far, other, j):
    x = 1 - pos[0] if far else pos[0]
    core = 1 - pos[1] if other else pos[1]
    return pl.multiple_of(((x * Y + j) * CORE + core) * LANES, LANES)


def lay_out(pos, parts, whole):
    for j in range(Y):
        for other, part in enumerate(parts):
            at = pl.multiple_of((j * CORE + (1 - pos[1] if other else pos[1])) * LANES, LANES)
            whole[:, pl.ds(at, LANES)] = part[j]


def side(pos, far):
    x = 1 - pos[0] if far else pos[0]
    return pl.multiple_of(x * (Y * CORE * LANES), LANES)


def pack(pos, w, ow, sent_w, sent_ow):
    for far in range(2):
        for j in range(Y):
            off = offset(pos, far, 1, j)
            for b in range(3):
                sent_w[b, far * Y + j] = w[b, pl.ds(off, LANES), :].T
            sent_ow[far * Y + j] = ow[:, pl.ds(off, LANES)]


def turn(pos, w, own):
    for far in range(2):
        for j in range(Y):
            off = offset(pos, far, 0, j)
            for b in range(3):
                own[b, far * Y + j] = w[b, pl.ds(off, LANES), :].T


def project_side(pos, far, t0, t1, w, whole):
    lay_out(pos, (t0, t1), whole)
    rows = pl.ds(side(pos, far), whole.shape[1])
    rhs = jnp.concatenate([w[b, rows, :] for b in range(3)], axis=1)
    return jnp.dot(whole[...], rhs, preferred_element_type=F32)


def project_near(pos, t0, t1, w, near, whole):
    near[...] = project_side(pos, 0, t0, t1, w, whole)


def project(pos, t2, t3, near, w, q, k, v, mix, tail, whole):
    proj = (near[...] + project_side(pos, 1, t2, t3, w, whole)).astype(BF)
    q[...] = proj[:, :LANES]
    k[...] = proj[:, LANES : 2 * LANES]
    v[...] = proj[:, 2 * LANES :]
    product = (f32(proj[:, LANES : 2 * LANES]) * f32(proj[:, 2 * LANES :])).astype(BF)
    mix[...] = product
    tail[...] = product[-tail.shape[0] :]


def shift_all(ext, shifted, back):
    total = ext.shape[0]
    for b in range(8):
        by = (total - b) % total if back else b
        shifted[b] = pltpu.roll(ext, by, 0) if by else ext


def strip_sum(at, zero, first, last, limit, taps, shifted, back):
    lim = limit[at : at + STRIP, :]

    def eight(a, acc):
        start = pl.multiple_of(zero + 8 * a if back else zero - 8 * a, 8)
        for b in range(8):
            s = 8 * a + b
            piece = shifted[b, pl.ds(start, STRIP), :]
            acc = acc + jnp.where(lim >= s, piece, 0.0) * taps[pl.ds(s, 1), :]
        return acc

    return lax.fori_loop(first, last, eight, jnp.zeros((STRIP, LANES), F32))


def filtered_near(pos, mix, reach, taps, near, shifted):
    n_taps = taps.shape[0]
    shift_all(jnp.concatenate([jnp.zeros((n_taps, LANES), F32), f32(mix[...])], axis=0), shifted, False)
    for at in range(0, mix.shape[0], STRIP):
        last = min(n_taps, at + STRIP) // 8
        near[at : at + STRIP] = strip_sum(at, n_taps + at, 0, last, reach, taps, shifted, False)


def filtered(pos, prior, near, q, reach, taps, conv, gated, shifted):
    n_taps = taps.shape[0]
    shift_all(jnp.concatenate([f32(prior[...]), jnp.zeros((n_taps, LANES), F32)], axis=0), shifted, False)
    for at in range(0, conv.shape[0], STRIP):
        total = near[at : at + STRIP]
        if at < n_taps:
            total += strip_sum(at, n_taps + at, at // 8, n_taps // 8, reach, taps, shifted, False)
        conv[at : at + STRIP] = total
        gated[at : at + STRIP] = (f32(q[at : at + STRIP]) * total).astype(BF)


def slot(pos, far, j):
    return (1 - pos[0] if far else pos[0]) * Y + j


def out_terms(pos, mine, theirs, w, given, terms):
    both = jnp.concatenate([mine[...], theirs[...]], axis=1)
    for far in range(2):
        for j in range(0, Y, 2):
            rhs = jnp.concatenate(
                [
                    jnp.concatenate(
                        [w[:, pl.ds(offset(pos, far, 0, i), LANES)], given[far * Y + i]], axis=0
                    )
                    for i in (j, j + 1)
                ],
                axis=1,
            )
            term = jnp.dot(both, rhs, preferred_element_type=F32).astype(BF)
            terms[slot(pos, far, j)] = term[:, :LANES]
            terms[slot(pos, far, j + 1)] = term[:, LANES:]


def gate_side(pos, other, part, w, whole, weights):
    rows = whole.shape[0]
    for far in range(2):
        for j in range(Y):
            at = (far * Y + j) * LANES
            whole[:, at : at + LANES] = part[j, far * rows : (far + 1) * rows]
            weights[:, at : at + LANES] = w[:, pl.ds(offset(pos, far, other, j), LANES)]
    return lax.dot_general(
        whole[...], weights[...], (((1,), (1,)), ((), ())), preferred_element_type=F32
    )


def gate_near(pos, c0, w, near, whole, weights):
    near[...] = gate_side(pos, 0, c0, w, whole, weights)


def back_gate(pos, c1, near, w, q, dgated, dconv, head, whole, weights):
    total = near[...] + gate_side(pos, 1, c1, w, whole, weights)
    dgated[...] = total
    d = (total * f32(q[...])).astype(BF)
    dconv[...] = d
    head[...] = d[: head.shape[0]]


def back_near(pos, dconv, rem, taps, near, shifted):
    n_taps, rows = taps.shape[0], dconv.shape[0]
    shift_all(jnp.concatenate([f32(dconv[...]), jnp.zeros((n_taps, LANES), F32)], axis=0), shifted, True)
    for at in range(0, rows, STRIP):
        last = min(n_taps, rows - at) // 8
        near[at : at + STRIP] = strip_sum(at, at, 0, last, rem, taps, shifted, True)


def back_filtered(pos, after, near, k, v, dgated, conv, rem, taps, dproj, shifted):
    n_taps, rows = taps.shape[0], near.shape[0]
    shift_all(jnp.concatenate([jnp.zeros((n_taps, LANES), F32), f32(after[...])], axis=0), shifted, True)
    for at in range(0, rows, STRIP):
        here = slice(at, at + STRIP)
        dmix = near[here]
        left = rows - at - STRIP
        if left < n_taps:
            first = left // 8
            dmix += strip_sum(
                at, at - (rows - n_taps), first, n_taps // 8, rem, taps, shifted, True
            )
        dproj[here, :LANES] = (dgated[here] * conv[here]).astype(BF)
        dproj[here, LANES : 2 * LANES] = (dmix * f32(v[here])).astype(BF)
        dproj[here, 2 * LANES :] = (dmix * f32(k[here])).astype(BF)


def grad_terms(pos, mine, theirs, own, given, near, far_terms):
    both = jnp.concatenate([mine[...], theirs[...]], axis=1)
    for far, terms in ((1, far_terms), (0, near)):
        for j in range(0, Y, 2):
            rhs = jnp.concatenate(
                [
                    jnp.concatenate(
                        [own[b, far * Y + i] for b in range(3)]
                        + [given[b, far * Y + i] for b in range(3)],
                        axis=0,
                    )
                    for i in (j, j + 1)
                ],
                axis=1,
            )
            term = jnp.dot(both, rhs, preferred_element_type=F32).astype(BF)
            terms[j] = term[:, :LANES]
            terms[j + 1] = term[:, LANES:]


def passed_along(block, distance):
    devices = range(lax.axis_size("ctx"))
    route = [(i - distance, i) for i in devices if i - distance in devices]
    return lax.ppermute(block, "ctx", route)


def spread_y(block):
    copies = jnp.broadcast_to(block[None], (Y,) + block.shape)
    return lax.all_to_all(copies, "y", split_axis=0, concat_axis=0, tiled=True)


def swapped(block, axis):
    return lax.ppermute(block, axis, SWAP)


def summed(terms, axes):
    arrived = lax.all_to_all(terms, axes, split_axis=0, concat_axis=0, tiled=True)
    return f32(arrived).sum(axis=0).astype(BF)


def block_step(tokens, cotangent, in_weight, filter_taps, out_weight, segment_ids):
    width, _, chans = in_weight.shape
    rows = tokens.shape[0]
    taps = filter_taps.shape[0]
    n_chips = X * Y
    block, edge, triple = (rows, chans), (taps, chans), (rows, 3 * chans)
    weights = [pltpu.VMEM((chans, width // 2), BF)]
    half = [pltpu.VMEM((rows, width // 2), BF)]
    long = [pltpu.VMEM((8, rows + taps, chans), F32)]
    short = [pltpu.VMEM((8, 2 * taps, chans), F32)]
    macs = rows * width * chans
    small = rows * width * 2

    w3 = in_weight.transpose(1, 0, 2)
    pos = jnp.stack([lax.axis_index("x"), lax.axis_index("core")]).astype(jnp.int32)
    t0 = spread_y(tokens)
    far_cot = swapped(cotangent, "x")
    sent_w, sent_ow = call(
        pack,
        [((3, n_chips, chans, LANES), BF), ((n_chips, chans, LANES), BF)], [],
        macs, 4 * small, pos, w3, out_weight,
    )
    given_w = swapped(sent_w, "core")
    given_ow = swapped(sent_ow, "core")
    (own_w,) = call(turn, [((3, n_chips, chans, LANES), BF)], [], macs, 4 * small, pos, w3)
    base = lax.axis_index("ctx") * rows
    positions = base + jnp.arange(rows, dtype=jnp.int32)
    seg_here = lax.dynamic_slice_in_dim(segment_ids, base, rows)
    first = jnp.sum((segment_ids[None, :] < seg_here[:, None]).astype(jnp.int32), axis=1)
    end = jnp.sum((segment_ids[None, :] <= seg_here[:, None]).astype(jnp.int32), axis=1)
    reach = jnp.broadcast_to((positions - first)[:, None], block)
    rem = jnp.broadcast_to((end - 1 - positions)[:, None], block)

    c0 = spread_y(jnp.concatenate([cotangent, far_cot], axis=0))
    t2 = swapped(t0, "x")
    t1 = swapped(t0, "core")
    t3 = swapped(t2, "core")
    c1 = swapped(c0, "core")

    (near,) = call(project_near, [(triple, F32)], half, 3 * macs, 2 * small, pos, t0, t1, w3)
    q, k, v, mix, tail = call(
        project, [(block, BF)] * 4 + [(edge, BF)], half,
        3 * macs, 2 * small, pos, t2, t3, near, w3,
    )
    prior = passed_along(tail, 1)
    (near,) = call(
        filtered_near, [(block, F32)], long,
        macs, small, pos, mix, reach, filter_taps,
    )
    conv, gated = call(
        filtered, [(block, F32), (block, BF)], short,
        macs // 2, small // 2, pos, prior, near, q, reach, filter_taps,
    )
    theirs = swapped(gated, "core")
    (terms,) = call(
        out_terms, [((n_chips, rows, LANES), BF)], [],
        2 * macs, 2 * small, pos, gated, theirs, out_weight, given_ow,
    )
    block_out = summed(terms, ("x", "y"))
    (near,) = call(gate_near, [(block, F32)], half + weights, macs, small, pos, c0, out_weight)
    dgated, dconv, head = call(
        back_gate, [(block, F32), (block, BF), (edge, BF)], half + weights,
        macs, small, pos, c1, near, out_weight, q,
    )
    after = passed_along(head, -1)
    (near,) = call(back_near, [(block, F32)], long, macs, small, pos, dconv, rem, filter_taps)
    (dproj,) = call(
        back_filtered, [(triple, BF)], short,
        macs // 2, small // 2, pos, after, near, k, v, dgated, conv, rem, filter_taps,
    )
    theirs = swapped(dproj, "core")
    near, far = call(
        grad_terms, [((Y, rows, LANES), BF)] * 2, [],
        6 * macs, 4 * small, pos, dproj, theirs, own_w, given_w,
    )
    got = swapped(far, "x")
    return block_out, summed((f32(near) + f32(got)).astype(BF), "y")


def solution(mesh):
    fine = Mesh(
        mesh.devices.reshape(mesh.shape["ctx"], X, Y, CORE), ("ctx", "x", "y", "core")
    )
    tp = ("x", "y", "core")
    placed = (P("ctx", tp), P("ctx", tp), P(None, None, tp), P(None, tp), P(tp, None), P())
    return jax.shard_map(
        block_step,
        mesh=fine,
        in_specs=placed,
        out_specs=(P("ctx", tp), P("ctx", tp)),
        check_vma=False,
    )
```

```python
import jax
import jax.numpy as jnp
from jax import lax
from jax.experimental import pallas as pl
from jax.experimental.pallas import tpu as pltpu
from jax.sharding import Mesh
from jax.sharding import PartitionSpec as P

X, Y, CORE = 2, 8, 2
SWAP = [(0, 1), (1, 0)]
LANES = 128
STRIP = 64
INTERPRET = False
BF, F32 = jnp.bfloat16, jnp.float32


def f32(a):
    return a.astype(F32)


def call(kernel, outs, scratch, flops, nbytes, *args):
    return pl.pallas_call(
        kernel,
        out_shape=[jax.ShapeDtypeStruct(s, d) for s, d in outs],
        in_specs=[pl.BlockSpec(memory_space=pltpu.SMEM)]
        + [pl.BlockSpec(memory_space=pltpu.VMEM)] * (len(args) - 1),
        out_specs=[pl.BlockSpec(memory_space=pltpu.VMEM)] * len(outs),
        scratch_shapes=scratch,
        cost_estimate=pl.CostEstimate(flops=flops, bytes_accessed=nbytes, transcendentals=0),
        compiler_params=pltpu.CompilerParams(vmem_limit_bytes=48 << 20),
        interpret=INTERPRET,
    )(*args)


def offset(pos, far, other, j):
    x = 1 - pos[0] if far else pos[0]
    core = 1 - pos[1] if other else pos[1]
    return pl.multiple_of(((x * Y + j) * CORE + core) * LANES, LANES)


def lay_out(pos, parts, whole):
    for j in range(Y):
        for other, part in enumerate(parts):
            at = pl.multiple_of((j * CORE + (1 - pos[1] if other else pos[1])) * LANES, LANES)
            whole[:, pl.ds(at, LANES)] = part[j]


def side(pos, far):
    x = 1 - pos[0] if far else pos[0]
    return pl.multiple_of(x * (Y * CORE * LANES), LANES)


def pack(pos, w, ow, sent_w, sent_ow):
    for far in range(2):
        for j in range(Y):
            off = offset(pos, far, 1, j)
            for b in range(3):
                sent_w[b, far * Y + j] = w[b, pl.ds(off, LANES), :].T
            sent_ow[far * Y + j] = ow[:, pl.ds(off, LANES)]


def turn(pos, w, own):
    for far in range(2):
        for j in range(Y):
            off = offset(pos, far, 0, j)
            for b in range(3):
                own[b, far * Y + j] = w[b, pl.ds(off, LANES), :].T


def project_side(pos, far, t0, t1, w, whole):
    lay_out(pos, (t0, t1), whole)
    rows = pl.ds(side(pos, far), whole.shape[1])
    rhs = jnp.concatenate([w[b, rows, :] for b in range(3)], axis=1)
    return jnp.dot(whole[...], rhs, preferred_element_type=F32)


def project_near(pos, t0, t1, w, near, whole):
    near[...] = project_side(pos, 0, t0, t1, w, whole)


def project(pos, t2, t3, near, w, q, k, v, mix, tail, whole):
    proj = (near[...] + project_side(pos, 1, t2, t3, w, whole)).astype(BF)
    q[...] = proj[:, :LANES]
    k[...] = proj[:, LANES : 2 * LANES]
    v[...] = proj[:, 2 * LANES :]
    product = (f32(proj[:, LANES : 2 * LANES]) * f32(proj[:, 2 * LANES :])).astype(BF)
    mix[...] = product
    tail[...] = product[-tail.shape[0] :]


def shift_all(ext, shifted, back):
    total = ext.shape[0]
    for b in range(8):
        by = (total - b) % total if back else b
        shifted[b] = pltpu.roll(ext, by, 0) if by else ext


def strip_sum(at, zero, first, last, limit, taps, shifted, back):
    lim = limit[at : at + STRIP, :]

    def eight(a, acc):
        start = pl.multiple_of(zero + 8 * a if back else zero - 8 * a, 8)
        for b in range(8):
            s = 8 * a + b
            piece = shifted[b, pl.ds(start, STRIP), :]
            acc = acc + jnp.where(lim >= s, piece, 0.0) * taps[pl.ds(s, 1), :]
        return acc

    return lax.fori_loop(first, last, eight, jnp.zeros((STRIP, LANES), F32))


def filtered_near(pos, mix, reach, taps, near, shifted):
    n_taps = taps.shape[0]
    shift_all(jnp.concatenate([jnp.zeros((n_taps, LANES), F32), f32(mix[...])], axis=0), shifted, False)
    for at in range(0, mix.shape[0], STRIP):
        last = min(n_taps, at + STRIP) // 8
        near[at : at + STRIP] = strip_sum(at, n_taps + at, 0, last, reach, taps, shifted, False)


def filtered(pos, prior, near, q, reach, taps, conv, gated, shifted):
    n_taps = taps.shape[0]
    shift_all(jnp.concatenate([f32(prior[...]), jnp.zeros((n_taps, LANES), F32)], axis=0), shifted, False)
    for at in range(0, conv.shape[0], STRIP):
        total = near[at : at + STRIP]
        if at < n_taps:
            total += strip_sum(at, n_taps + at, at // 8, n_taps // 8, reach, taps, shifted, False)
        conv[at : at + STRIP] = total
        gated[at : at + STRIP] = (f32(q[at : at + STRIP]) * total).astype(BF)


def out_terms(pos, mine, theirs, w, given, near, far_terms):
    both = jnp.concatenate([mine[...], theirs[...]], axis=1)
    for far, terms in ((1, far_terms), (0, near)):
        for j in range(0, Y, 2):
            rhs = jnp.concatenate(
                [
                    jnp.concatenate(
                        [w[:, pl.ds(offset(pos, far, 0, i), LANES)], given[far * Y + i]], axis=0
                    )
                    for i in (j, j + 1)
                ],
                axis=1,
            )
            term = jnp.dot(both, rhs, preferred_element_type=F32).astype(BF)
            terms[j] = term[:, :LANES]
            terms[j + 1] = term[:, LANES:]


def fold(pos, near, got, *by_distance):
    for d, out in enumerate(by_distance):
        at = lax.rem(pos[2] + d, Y)
        out[...] = (f32(near[at]) + f32(got[at])).astype(BF)


def gate_side(pos, other, part, w, whole, weights):
    rows = whole.shape[0]
    for far in range(2):
        for j in range(Y):
            at = (far * Y + j) * LANES
            whole[:, at : at + LANES] = part[j, far * rows : (far + 1) * rows]
            weights[:, at : at + LANES] = w[:, pl.ds(offset(pos, far, other, j), LANES)]
    return lax.dot_general(
        whole[...], weights[...], (((1,), (1,)), ((), ())), preferred_element_type=F32
    )


def gate_near(pos, c0, w, near, whole, weights):
    near[...] = gate_side(pos, 0, c0, w, whole, weights)


def back_gate(pos, c1, near, w, q, dgated, dconv, head, whole, weights):
    total = near[...] + gate_side(pos, 1, c1, w, whole, weights)
    dgated[...] = total
    d = (total * f32(q[...])).astype(BF)
    dconv[...] = d
    head[...] = d[: head.shape[0]]


def back_near(pos, dconv, rem, taps, near, shifted):
    n_taps, rows = taps.shape[0], dconv.shape[0]
    shift_all(jnp.concatenate([f32(dconv[...]), jnp.zeros((n_taps, LANES), F32)], axis=0), shifted, True)
    for at in range(0, rows, STRIP):
        last = min(n_taps, rows - at) // 8
        near[at : at + STRIP] = strip_sum(at, at, 0, last, rem, taps, shifted, True)


def back_filtered(pos, after, near, k, v, dgated, conv, rem, taps, dproj, shifted):
    n_taps, rows = taps.shape[0], near.shape[0]
    shift_all(jnp.concatenate([jnp.zeros((n_taps, LANES), F32), f32(after[...])], axis=0), shifted, True)
    for at in range(0, rows, STRIP):
        here = slice(at, at + STRIP)
        dmix = near[here]
        left = rows - at - STRIP
        if left < n_taps:
            first = left // 8
            dmix += strip_sum(
                at, at - (rows - n_taps), first, n_taps // 8, rem, taps, shifted, True
            )
        dproj[here, :LANES] = (dgated[here] * conv[here]).astype(BF)
        dproj[here, LANES : 2 * LANES] = (dmix * f32(v[here])).astype(BF)
        dproj[here, 2 * LANES :] = (dmix * f32(k[here])).astype(BF)


def grad_terms(pos, mine, theirs, own, given, terms, far):
    both = jnp.concatenate([mine[...], theirs[...]], axis=1)
    for j in range(0, Y, 2):
        rhs = jnp.concatenate(
            [
                jnp.concatenate(
                    [own[b, far * Y + i] for b in range(3)]
                    + [given[b, far * Y + i] for b in range(3)],
                    axis=0,
                )
                for i in (j, j + 1)
            ],
            axis=1,
        )
        term = jnp.dot(both, rhs, preferred_element_type=F32).astype(BF)
        terms[j] = term[:, :LANES]
        terms[j + 1] = term[:, LANES:]


def grad_far(*refs):
    grad_terms(*refs, 1)


def grad_near(*refs):
    grad_terms(*refs, 0)


def passed_along(block, distance):
    devices = range(lax.axis_size("ctx"))
    route = [(i - distance, i) for i in devices if i - distance in devices]
    return lax.ppermute(block, "ctx", route)


def spread_y(block):
    copies = jnp.broadcast_to(block[None], (Y,) + block.shape)
    return lax.all_to_all(copies, "y", split_axis=0, concat_axis=0, tiled=True)


def swapped(block, axis):
    return lax.ppermute(block, axis, SWAP)


def summed(terms):
    arrived = lax.all_to_all(terms, "y", split_axis=0, concat_axis=0, tiled=True)
    return f32(arrived).sum(axis=0).astype(BF)


def summed_by_steps(by_distance):
    total = f32(by_distance[0])
    for d in (4, 3, 5, 2, 6, 1, 7):
        got = lax.ppermute(by_distance[d], "y", [(i, (i + d) % Y) for i in range(Y)])
        total += f32(got)
    return total.astype(BF)


def block_step(tokens, cotangent, in_weight, filter_taps, out_weight, segment_ids):
    width, _, chans = in_weight.shape
    rows = tokens.shape[0]
    taps = filter_taps.shape[0]
    n_chips = X * Y
    block, edge, triple = (rows, chans), (taps, chans), (rows, 3 * chans)
    weights = [pltpu.VMEM((chans, width // 2), BF)]
    half = [pltpu.VMEM((rows, width // 2), BF)]
    long = [pltpu.VMEM((8, rows + taps, chans), F32)]
    short = [pltpu.VMEM((8, 2 * taps, chans), F32)]
    macs = rows * width * chans
    small = rows * width * 2

    w3 = in_weight.transpose(1, 0, 2)
    pos = jnp.stack([lax.axis_index(n) for n in ("x", "core", "y")]).astype(jnp.int32)
    t0 = spread_y(tokens)
    far_cot = swapped(cotangent, "x")
    sent_w, sent_ow = call(
        pack,
        [((3, n_chips, chans, LANES), BF), ((n_chips, chans, LANES), BF)], [],
        macs, 4 * small, pos, w3, out_weight,
    )
    given_w = swapped(sent_w, "core")
    given_ow = swapped(sent_ow, "core")
    (own_w,) = call(turn, [((3, n_chips, chans, LANES), BF)], [], macs, 4 * small, pos, w3)
    base = lax.axis_index("ctx") * rows
    positions = base + jnp.arange(rows, dtype=jnp.int32)
    seg_here = lax.dynamic_slice_in_dim(segment_ids, base, rows)
    first = jnp.sum((segment_ids[None, :] < seg_here[:, None]).astype(jnp.int32), axis=1)
    end = jnp.sum((segment_ids[None, :] <= seg_here[:, None]).astype(jnp.int32), axis=1)
    reach = jnp.broadcast_to((positions - first)[:, None], block)
    rem = jnp.broadcast_to((end - 1 - positions)[:, None], block)

    c0 = spread_y(jnp.concatenate([cotangent, far_cot], axis=0))
    t2 = swapped(t0, "x")
    t1 = swapped(t0, "core")
    t3 = swapped(t2, "core")
    c1 = swapped(c0, "core")

    (near,) = call(project_near, [(triple, F32)], half, 3 * macs, 2 * small, pos, t0, t1, w3)
    q, k, v, mix, tail = call(
        project, [(block, BF)] * 4 + [(edge, BF)], half,
        3 * macs, 2 * small, pos, t2, t3, near, w3,
    )
    prior = passed_along(tail, 1)
    (near,) = call(
        filtered_near, [(block, F32)], long,
        macs, small, pos, mix, reach, filter_taps,
    )
    conv, gated = call(
        filtered, [(block, F32), (block, BF)], short,
        macs // 2, small // 2, pos, prior, near, q, reach, filter_taps,
    )
    theirs = swapped(gated, "core")
    near, far = call(
        out_terms, [((Y, rows, LANES), BF)] * 2, [],
        2 * macs, 2 * small, pos, gated, theirs, out_weight, given_ow,
    )
    got = swapped(far, "x")
    parts = call(fold, [(block, BF)] * Y, [], small, 2 * small, pos, near, got)
    block_out = summed_by_steps(parts)
    (near,) = call(gate_near, [(block, F32)], half + weights, macs, small, pos, c0, out_weight)
    dgated, dconv, head = call(
        back_gate, [(block, F32), (block, BF), (edge, BF)], half + weights,
        macs, small, pos, c1, near, out_weight, q,
    )
    after = passed_along(head, -1)
    (near,) = call(back_near, [(block, F32)], long, macs, small, pos, dconv, rem, filter_taps)
    (dproj,) = call(
        back_filtered, [(triple, BF)], short,
        macs // 2, small // 2, pos, after, near, k, v, dgated, conv, rem, filter_taps,
    )
    theirs = swapped(dproj, "core")
    weights = (dproj, theirs, own_w, given_w)
    (far,) = call(grad_far, [((Y, rows, LANES), BF)], [], 3 * macs, 2 * small, pos, *weights)
    got = swapped(far, "x")
    (near,) = call(grad_near, [((Y, rows, LANES), BF)], [], 3 * macs, 2 * small, pos, *weights)
    return block_out, summed((f32(near) + f32(got)).astype(BF))


def solution(mesh):
    fine = Mesh(
        mesh.devices.reshape(mesh.shape["ctx"], X, Y, CORE), ("ctx", "x", "y", "core")
    )
    tp = ("x", "y", "core")
    placed = (P("ctx", tp), P("ctx", tp), P(None, None, tp), P(None, tp), P(tp, None), P())
    return jax.shard_map(
        block_step,
        mesh=fine,
        in_specs=placed,
        out_specs=(P("ctx", tp), P("ctx", tp)),
        check_vma=False,
    )
```

```python
import jax
import jax.numpy as jnp
from jax import lax
from jax.experimental import pallas as pl
from jax.experimental.pallas import tpu as pltpu
from jax.sharding import Mesh
from jax.sharding import PartitionSpec as P

X, Y, CORE = 2, 8, 2
SWAP = [(0, 1), (1, 0)]
LANES = 128
STRIP = 64
INTERPRET = False
BF, F32 = jnp.bfloat16, jnp.float32


def f32(a):
    return a.astype(F32)


def call(kernel, outs, scratch, flops, nbytes, *args):
    return pl.pallas_call(
        kernel,
        out_shape=[jax.ShapeDtypeStruct(s, d) for s, d in outs],
        in_specs=[pl.BlockSpec(memory_space=pltpu.SMEM)]
        + [pl.BlockSpec(memory_space=pltpu.VMEM)] * (len(args) - 1),
        out_specs=[pl.BlockSpec(memory_space=pltpu.VMEM)] * len(outs),
        scratch_shapes=scratch,
        cost_estimate=pl.CostEstimate(flops=flops, bytes_accessed=nbytes, transcendentals=0),
        compiler_params=pltpu.CompilerParams(vmem_limit_bytes=48 << 20),
        interpret=INTERPRET,
    )(*args)


def x_side(pos, far):
    return 1 - pos[0] if far else pos[0]


def core_side(pos, other):
    return 1 - pos[1] if other else pos[1]


def lanes(at):
    return pl.ds(pl.multiple_of(at * LANES, LANES), LANES)


def lay_out(pos, part, first, whole, start):
    rows = whole.shape[0]
    for j in range(Y):
        for other in range(2):
            at = first + other * rows
            to = start + j * CORE + core_side(pos, other)
            whole[:, lanes(to)] = part[j, at : at + rows]


def turn(pos, own, other, turned):
    span = turned.shape[3]
    for b in range(3):
        for o, w in enumerate((own, other)):
            for n in range(turned.shape[1]):
                turned[2 * b + o, n] = w[b, n * span : (n + 1) * span, :].T


def project_side(pos, far, part, own, other, whole):
    lay_out(pos, part, 0, whole, 0)
    depth = whole.shape[1]
    rows = pl.ds(pl.multiple_of(x_side(pos, far) * depth, depth), depth)
    rhs = jnp.concatenate([w[b, rows, :] for b in range(3) for w in (own, other)], axis=1)
    return jnp.dot(whole[...], rhs, preferred_element_type=F32)


def project_near(pos, part, own, other, near, whole):
    near[...] = project_side(pos, 0, part, own, other, whole)


def put(pos, value, out):
    for o in range(2):
        out[:, lanes(core_side(pos, o))] = value[:, o * LANES : (o + 1) * LANES]


def project(pos, part, near, own, other, q, k, v, mix, tail, whole):
    proj = (near[...] + project_side(pos, 1, part, own, other, whole)).astype(BF)
    wide = q.shape[1]
    key, value = proj[:, wide : 2 * wide], proj[:, 2 * wide :]
    q[...] = proj[:, :wide]
    k[...] = key
    v[...] = value
    product = (f32(key) * f32(value)).astype(BF)
    mix[...] = product
    put(pos, product, tail)


def shift_all(ext, shifted, back):
    total = ext.shape[0]
    for b in range(8):
        by = (total - b) % total if back else b
        shifted[b] = pltpu.roll(ext, by, 0) if by else ext


def strip_sum(at, zero, first, last, limit, taps, shifted, back):
    lim = limit[at : at + STRIP, :]

    def eight(a, acc):
        start = pl.multiple_of(zero + 8 * a if back else zero - 8 * a, 8)
        for b in range(8):
            s = 8 * a + b
            piece = shifted[b, pl.ds(start, STRIP), :]
            acc = acc + jnp.where(lim >= s, piece, 0.0) * taps[pl.ds(s, 1), :]
        return acc

    return lax.fori_loop(first, last, eight, jnp.zeros((STRIP, LANES), F32))


def filtered_near(pos, mix, reach, taps, taps_other, near, shifted):
    n_taps = taps.shape[0]
    for o, t in enumerate((taps, taps_other)):
        cols = slice(o * LANES, (o + 1) * LANES)
        shift_all(
            jnp.concatenate([jnp.zeros((n_taps, LANES), F32), f32(mix[:, cols])], axis=0),
            shifted, False,
        )
        for at in range(0, mix.shape[0], STRIP):
            last = min(n_taps, at + STRIP) // 8
            near[at : at + STRIP, cols] = strip_sum(
                at, n_taps + at, 0, last, reach, t, shifted, False
            )


def filtered(pos, prior, near, q, reach, taps, taps_other, conv, gated, shifted):
    n_taps = taps.shape[0]
    for o, t in enumerate((taps, taps_other)):
        cols = slice(o * LANES, (o + 1) * LANES)
        shift_all(
            jnp.concatenate(
                [f32(prior[:, lanes(core_side(pos, o))]), jnp.zeros((n_taps, LANES), F32)], axis=0
            ),
            shifted, False,
        )
        for at in range(0, conv.shape[0], STRIP):
            here = slice(at, at + STRIP)
            total = near[here, cols]
            if at < n_taps:
                total += strip_sum(
                    at, n_taps + at, at // 8, n_taps // 8, reach, t, shifted, False
                )
            conv[here, cols] = total
            gated[here, cols] = (f32(q[here, cols]) * total).astype(BF)


def out_terms(pos, gated, own, other, terms):
    span = terms.shape[2]
    for n in range(terms.shape[0]):
        cols = slice(n * span, (n + 1) * span)
        rhs = jnp.concatenate([own[:, cols], other[:, cols]], axis=0)
        terms[n] = jnp.dot(gated[...], rhs, preferred_element_type=F32).astype(BF)


def back_gate(pos, part, own, other, q, dgated, dconv, head, whole):
    rows = whole.shape[0]
    for far in range(2):
        lay_out(pos, part, 2 * far * rows, whole, x_side(pos, far) * (Y * CORE))
    total = lax.dot_general(
        whole[...],
        jnp.concatenate([own[...], other[...]], axis=0),
        (((1,), (1,)), ((), ())),
        preferred_element_type=F32,
    )
    dgated[...] = total
    d = (total * f32(q[...])).astype(BF)
    dconv[...] = d
    put(pos, d, head)


def back_near(pos, dconv, rem, taps, taps_other, near, shifted):
    n_taps, rows = taps.shape[0], dconv.shape[0]
    for o, t in enumerate((taps, taps_other)):
        cols = slice(o * LANES, (o + 1) * LANES)
        shift_all(
            jnp.concatenate([f32(dconv[:, cols]), jnp.zeros((n_taps, LANES), F32)], axis=0),
            shifted, True,
        )
        for at in range(0, rows, STRIP):
            last = min(n_taps, rows - at) // 8
            near[at : at + STRIP, cols] = strip_sum(at, at, 0, last, rem, t, shifted, True)


def back_filtered(pos, after, near, k, v, dgated, conv, rem, taps, taps_other, dproj, shifted):
    n_taps, (rows, wide) = taps.shape[0], near.shape
    for o, t in enumerate((taps, taps_other)):
        cols = slice(o * LANES, (o + 1) * LANES)
        shift_all(
            jnp.concatenate(
                [jnp.zeros((rows, LANES), F32), f32(after[:, lanes(core_side(pos, o))])], axis=0
            ),
            shifted, True,
        )
        for at in range(0, rows, STRIP):
            here = slice(at, at + STRIP)
            dmix = near[here, cols]
            left = rows - at - STRIP
            if left < n_taps:
                dmix += strip_sum(at, at, left // 8, n_taps // 8, rem, t, shifted, True)
            for b, d in enumerate(
                (dgated[here, cols] * conv[here, cols], dmix * f32(v[here, cols]), dmix * f32(k[here, cols]))
            ):
                at_col = b * wide + o * LANES
                dproj[here, at_col : at_col + LANES] = d.astype(BF)


def grad_terms(pos, dproj, turned, terms, far):
    for j in range(Y):
        n = x_side(pos, far) * Y + j
        rhs = jnp.concatenate([turned[i, n] for i in range(6)], axis=0)
        terms[j] = jnp.dot(dproj[...], rhs, preferred_element_type=F32).astype(BF)


def grad_far(*refs):
    grad_terms(*refs, 1)


def grad_near(*refs):
    grad_terms(*refs, 0)


def add_up(pos, arrived, keep, give):
    total = f32(arrived[0])
    for n in range(1, arrived.shape[0]):
        total += f32(arrived[n])
    total = total.astype(BF)
    for core in range(2):
        part = total[:, core * LANES : (core + 1) * LANES]

        @pl.when(pos[1] == core)
        def _():
            keep[...] = part

        @pl.when(pos[1] != core)
        def _():
            give[...] = part


def join(pos, keep, got, out):
    rows = keep.shape[0]
    for other, part in enumerate((keep, got)):
        out[pl.ds(pl.multiple_of(core_side(pos, other) * rows, rows), rows), :] = part[...]


def passed_along(block, distance):
    devices = range(lax.axis_size("ctx") * CORE)
    route = [(i - distance, i) for i in devices if i - distance in devices]
    return lax.ppermute(block, ("ctx", "core"), route)


def spread_y(block):
    copies = jnp.broadcast_to(block[None], (Y,) + block.shape)
    return lax.all_to_all(copies, "y", split_axis=0, concat_axis=0, tiled=True)


def swapped(block, axis):
    return lax.ppermute(block, axis, SWAP)


def summed(terms, axes, pos, rows):
    arrived = lax.all_to_all(terms, axes, split_axis=0, concat_axis=0, tiled=True)
    size = terms.size
    keep, give = call(add_up, [((rows // CORE, LANES), BF)] * 2, [], size, 2 * size, pos, arrived)
    got = swapped(give, "core")
    (out,) = call(join, [((rows, LANES), BF)], [], 0, 4 * rows * LANES, pos, keep, got)
    return out


def block_step(tokens, cotangent, in_weight, filter_taps, out_weight, segment_ids):
    width, _, chans = in_weight.shape
    rows, taps = tokens.shape[0], filter_taps.shape[0]
    part, wide, n_chips = rows // CORE, CORE * chans, X * Y
    block, triple, narrow = (part, wide), (part, 3 * wide), (part, chans)
    whole = [pltpu.VMEM((part, width), BF)]
    half = [pltpu.VMEM((part, width // 2), BF)]
    shifted = [pltpu.VMEM((8, part + taps, LANES), F32)]
    macs = rows * width * chans
    small = rows * width * 2

    core = lax.axis_index("core")
    pos = jnp.stack([lax.axis_index("x"), core]).astype(jnp.int32)
    w3 = in_weight.transpose(1, 0, 2)

    def rows_of(a, which):
        return lax.dynamic_slice_in_dim(a, which * part, part, 0)

    sent = jnp.concatenate([rows_of(tokens, 1 - core), rows_of(cotangent, 1 - core)])
    got = swapped(sent, "core")
    tok = jnp.concatenate([rows_of(tokens, core), got[:part]])
    cot = jnp.concatenate([rows_of(cotangent, core), got[part:]])
    t0 = spread_y(tok)
    far_cot = swapped(cot, "x")
    w_other = swapped(w3, "core")
    ow_other = swapped(out_weight, "core")
    taps_other = swapped(filter_taps, "core")
    both_taps = (filter_taps, taps_other)
    base = lax.axis_index("ctx") * rows + core * part
    positions = base + jnp.arange(part, dtype=jnp.int32)
    seg_here = lax.dynamic_slice_in_dim(segment_ids, base, part)
    first = jnp.sum((segment_ids[None, :] < seg_here[:, None]).astype(jnp.int32), axis=1)
    end = jnp.sum((segment_ids[None, :] <= seg_here[:, None]).astype(jnp.int32), axis=1)
    reach = jnp.broadcast_to((positions - first)[:, None], narrow)
    rem = jnp.broadcast_to((end - 1 - positions)[:, None], narrow)
    t2 = swapped(t0, "x")
    c0 = spread_y(jnp.concatenate([cot, far_cot]))

    (turned,) = call(turn, [((6, n_chips, chans, wide), BF)], [], macs, 8 * small, pos, w3, w_other)
    (near,) = call(
        project_near, [(triple, F32)], half, 3 * macs, 2 * small,
        pos, t0, w3, w_other,
    )
    q, k, v, mix, tail = call(
        project, [(block, BF)] * 5, half, 3 * macs, 2 * small,
        pos, t2, near, w3, w_other,
    )
    prior = passed_along(tail, 1)
    (near,) = call(
        filtered_near, [(block, F32)], shifted, macs, small,
        pos, mix, reach, *both_taps,
    )
    conv, gated = call(
        filtered, [(block, F32), (block, BF)], shifted, macs, small // 2,
        pos, prior, near, q, reach, *both_taps,
    )
    (terms,) = call(
        out_terms, [((n_chips, part, wide), BF)], [], 2 * macs, 2 * small,
        pos, gated, out_weight, ow_other,
    )
    block_out = summed(terms, ("x", "y"), pos, rows)
    dgated, dconv, head = call(
        back_gate, [(block, F32), (block, BF), (block, BF)], whole, 2 * macs, small,
        pos, c0, out_weight, ow_other, q,
    )
    after = passed_along(head, -1)
    (near,) = call(back_near, [(block, F32)], shifted, macs, small, pos, dconv, rem, *both_taps)
    (dproj,) = call(
        back_filtered, [(triple, BF)], shifted, macs, small // 2,
        pos, after, near, k, v, dgated, conv, rem, *both_taps,
    )
    sides = [((Y, part, wide), BF)]
    (far,) = call(grad_far, sides, [], 3 * macs, 2 * small, pos, dproj, turned)
    got = swapped(far, "x")
    (near,) = call(grad_near, sides, [], 3 * macs, 2 * small, pos, dproj, turned)
    return block_out, summed((f32(near) + f32(got)).astype(BF), "y", pos, rows)


def solution(mesh):
    fine = Mesh(
        mesh.devices.reshape(mesh.shape["ctx"], X, Y, CORE), ("ctx", "x", "y", "core")
    )
    tp = ("x", "y", "core")
    placed = (P("ctx", tp), P("ctx", tp), P(None, None, tp), P(None, tp), P(tp, None), P())
    return jax.shard_map(
        block_step,
        mesh=fine,
        in_specs=placed,
        out_specs=(P("ctx", tp), P("ctx", tp)),
        check_vma=False,
    )
```

```python
import jax
import jax.numpy as jnp
from jax import lax
from jax.experimental import pallas as pl
from jax.experimental.pallas import tpu as pltpu
from jax.sharding import Mesh
from jax.sharding import PartitionSpec as P

X, Y, CORE = 2, 8, 2
SWAP = [(0, 1), (1, 0)]
LANES = 128
STRIP = 64
INTERPRET = False
BF, F32 = jnp.bfloat16, jnp.float32


def f32(a):
    return a.astype(F32)


def call(kernel, outs, scratch, flops, nbytes, *args):
    return pl.pallas_call(
        kernel,
        out_shape=[jax.ShapeDtypeStruct(s, d) for s, d in outs],
        in_specs=[pl.BlockSpec(memory_space=pltpu.SMEM)]
        + [pl.BlockSpec(memory_space=pltpu.VMEM)] * (len(args) - 1),
        out_specs=[pl.BlockSpec(memory_space=pltpu.VMEM)] * len(outs),
        scratch_shapes=scratch,
        cost_estimate=pl.CostEstimate(flops=flops, bytes_accessed=nbytes, transcendentals=0),
        compiler_params=pltpu.CompilerParams(vmem_limit_bytes=48 << 20),
        interpret=INTERPRET,
    )(*args)


def x_side(pos, far):
    return 1 - pos[0] if far else pos[0]


def core_side(pos, other):
    return 1 - pos[1] if other else pos[1]


def lanes(at):
    return pl.ds(pl.multiple_of(at * LANES, LANES), LANES)


def lay_out(part, first, whole, start):
    for n in range(part.shape[0]):
        whole[:, lanes(start + n)] = part[n, first : first + whole.shape[0]]


def turn(pos, w, near, far):
    span = near.shape[3]
    for side, out in ((0, near), (1, far)):
        for b in range(3):
            for j in range(Y):
                at = pl.multiple_of((x_side(pos, side) * Y + j) * span, span)
                out[b, j] = w[b, pl.ds(at, span), :].T


def project_side(pos, far, part, own, other, whole):
    for n in range(part.shape[0]):
        whole[:, n * LANES : (n + 1) * LANES] = part[n]
    depth = whole.shape[1]
    rows = pl.ds(pl.multiple_of(x_side(pos, far) * depth, depth), depth)
    rhs = jnp.concatenate([w[b, rows, :] for b in range(3) for w in (own, other)], axis=1)
    return jnp.dot(whole[...], rhs, preferred_element_type=F32)


def project_near(pos, part, own, other, near, whole):
    near[...] = project_side(pos, 0, part, own, other, whole)


def put(pos, value, out):
    for o in range(2):
        out[:, lanes(core_side(pos, o))] = value[:, o * LANES : (o + 1) * LANES]


def project(pos, part, near, own, other, q, k, v, mix, tail, whole):
    proj = (near[...] + project_side(pos, 1, part, own, other, whole)).astype(BF)
    wide = q.shape[1]
    key, value = proj[:, wide : 2 * wide], proj[:, 2 * wide :]
    q[...] = proj[:, :wide]
    k[...] = key
    v[...] = value
    product = (f32(key) * f32(value)).astype(BF)
    mix[...] = product
    put(pos, product, tail)


def shift_all(ext, shifted, back):
    total = ext.shape[0]
    for b in range(8):
        by = (total - b) % total if back else b
        shifted[b] = pltpu.roll(ext, by, 0) if by else ext


def strip_sum(at, zero, first, last, limit, taps, shifted, back):
    lim = limit[at : at + STRIP, :]

    def eight(a, acc):
        start = pl.multiple_of(zero + 8 * a if back else zero - 8 * a, 8)
        for b in range(8):
            s = 8 * a + b
            piece = shifted[b, pl.ds(start, STRIP), :]
            acc = acc + jnp.where(lim >= s, piece, 0.0) * taps[pl.ds(s, 1), :]
        return acc

    return lax.fori_loop(first, last, eight, jnp.zeros((STRIP, LANES), F32))


def filtered_near(pos, mix, reach, taps, taps_other, near, shifted):
    n_taps = taps.shape[0]
    for o, t in enumerate((taps, taps_other)):
        cols = slice(o * LANES, (o + 1) * LANES)
        shift_all(
            jnp.concatenate([jnp.zeros((n_taps, LANES), F32), f32(mix[:, cols])], axis=0),
            shifted, False,
        )
        for at in range(0, mix.shape[0], STRIP):
            last = min(n_taps, at + STRIP) // 8
            near[at : at + STRIP, cols] = strip_sum(
                at, n_taps + at, 0, last, reach, t, shifted, False
            )


def filtered(pos, prior, near, q, reach, taps, taps_other, conv, gated, shifted):
    n_taps = taps.shape[0]
    for o, t in enumerate((taps, taps_other)):
        cols = slice(o * LANES, (o + 1) * LANES)
        shift_all(
            jnp.concatenate(
                [f32(prior[:, lanes(core_side(pos, o))]), jnp.zeros((n_taps, LANES), F32)], axis=0
            ),
            shifted, False,
        )
        for at in range(0, conv.shape[0], STRIP):
            here = slice(at, at + STRIP)
            total = near[here, cols]
            if at < n_taps:
                total += strip_sum(
                    at, n_taps + at, at // 8, n_taps // 8, reach, t, shifted, False
                )
            conv[here, cols] = total
            gated[here, cols] = (f32(q[here, cols]) * total).astype(BF)


def out_terms(pos, gated, own, other, terms):
    span = CORE * LANES
    for n in range(0, terms.shape[0], CORE):
        cols = slice(n * LANES, n * LANES + span)
        rhs = jnp.concatenate([own[:, cols], other[:, cols]], axis=0)
        term = jnp.dot(gated[...], rhs, preferred_element_type=F32).astype(BF)
        for core in range(CORE):
            terms[n + core] = term[:, core * LANES : (core + 1) * LANES]


def back_gate(pos, part, own, other, q, dgated, dconv, head, whole):
    rows = whole.shape[0]
    for far in range(2):
        lay_out(part, far * rows, whole, x_side(pos, far) * (Y * CORE))
    total = lax.dot_general(
        whole[...],
        jnp.concatenate([own[...], other[...]], axis=0),
        (((1,), (1,)), ((), ())),
        preferred_element_type=F32,
    )
    dgated[...] = total
    d = (total * f32(q[...])).astype(BF)
    dconv[...] = d
    put(pos, d, head)


def back_near(pos, dconv, rem, taps, taps_other, near, shifted):
    n_taps, rows = taps.shape[0], dconv.shape[0]
    for o, t in enumerate((taps, taps_other)):
        cols = slice(o * LANES, (o + 1) * LANES)
        shift_all(
            jnp.concatenate([f32(dconv[:, cols]), jnp.zeros((n_taps, LANES), F32)], axis=0),
            shifted, True,
        )
        for at in range(0, rows, STRIP):
            last = min(n_taps, rows - at) // 8
            near[at : at + STRIP, cols] = strip_sum(at, at, 0, last, rem, t, shifted, True)


def back_filtered(pos, after, near, k, v, dgated, conv, rem, taps, taps_other, dproj, shifted):
    n_taps, (rows, wide) = taps.shape[0], near.shape
    for o, t in enumerate((taps, taps_other)):
        cols = slice(o * LANES, (o + 1) * LANES)
        shift_all(
            jnp.concatenate(
                [jnp.zeros((rows, LANES), F32), f32(after[:, lanes(core_side(pos, o))])], axis=0
            ),
            shifted, True,
        )
        for at in range(0, rows, STRIP):
            here = slice(at, at + STRIP)
            dmix = near[here, cols]
            left = rows - at - STRIP
            if left < n_taps:
                dmix += strip_sum(at, at, left // 8, n_taps // 8, rem, t, shifted, True)
            for b, d in enumerate(
                (dgated[here, cols] * conv[here, cols], dmix * f32(v[here, cols]), dmix * f32(k[here, cols]))
            ):
                at_col = b * wide + o * LANES
                dproj[here, at_col : at_col + LANES] = d.astype(BF)


def grad_terms(pos, dproj, own, other, terms):
    for j in range(Y):
        rhs = jnp.concatenate([w[b, j] for b in range(3) for w in (own, other)], axis=0)
        term = jnp.dot(dproj[...], rhs, preferred_element_type=F32).astype(BF)
        for core in range(CORE):
            terms[CORE * j + core] = term[:, core * LANES : (core + 1) * LANES]


def passed_along(block, distance):
    devices = range(lax.axis_size("ctx") * CORE)
    route = [(i - distance, i) for i in devices if i - distance in devices]
    return lax.ppermute(block, ("ctx", "core"), route)


def spread(halves):
    copies = jnp.broadcast_to(halves[None], (Y,) + halves.shape)
    copies = copies.reshape((Y * CORE,) + halves.shape[1:])
    return lax.all_to_all(copies, ("y", "core"), split_axis=0, concat_axis=0, tiled=True)


def swapped(block, axis):
    return lax.ppermute(block, axis, SWAP)


def summed(terms, axes):
    arrived = lax.all_to_all(terms, axes, split_axis=0, concat_axis=0, tiled=True)
    n, part, cols = arrived.shape
    return f32(arrived.reshape(n // CORE, CORE * part, cols)).sum(axis=0).astype(BF)


def block_step(tokens, cotangent, in_weight, filter_taps, out_weight, segment_ids):
    width, _, chans = in_weight.shape
    rows, taps = tokens.shape[0], filter_taps.shape[0]
    part, wide, n_chips = rows // CORE, CORE * chans, X * Y
    block, triple, narrow = (part, wide), (part, 3 * wide), (part, chans)
    whole = [pltpu.VMEM((part, width), BF)]
    half = [pltpu.VMEM((part, width // 2), BF)]
    shifted = [pltpu.VMEM((8, part + taps, LANES), F32)]
    macs = rows * width * chans
    small = rows * width * 2

    core = lax.axis_index("core")
    pos = jnp.stack([lax.axis_index("x"), core]).astype(jnp.int32)
    w3 = in_weight.transpose(1, 0, 2)

    t0 = spread(tokens.reshape(CORE, part, LANES))
    far_cot = swapped(cotangent, "x")
    w_other = swapped(w3, "core")
    ow_other = swapped(out_weight, "core")
    taps_other = swapped(filter_taps, "core")
    both_taps = (filter_taps, taps_other)
    base = lax.axis_index("ctx") * rows + core * part
    positions = base + jnp.arange(part, dtype=jnp.int32)
    seg_here = lax.dynamic_slice_in_dim(segment_ids, base, part)
    first = jnp.sum((segment_ids[None, :] < seg_here[:, None]).astype(jnp.int32), axis=1)
    end = jnp.sum((segment_ids[None, :] <= seg_here[:, None]).astype(jnp.int32), axis=1)
    reach = jnp.broadcast_to((positions - first)[:, None], narrow)
    rem = jnp.broadcast_to((end - 1 - positions)[:, None], narrow)
    t2 = swapped(t0, "x")
    both = [c.reshape(CORE, part, LANES) for c in (cotangent, far_cot)]
    c0 = spread(jnp.concatenate(both, axis=1))

    turned = [((3, Y, chans, wide), BF)] * 2
    other_near, other_far = call(turn, turned, [], macs, 4 * small, pos, w_other)
    (near,) = call(
        project_near, [(triple, F32)], half, 3 * macs, 2 * small,
        pos, t0, w3, w_other,
    )
    q, k, v, mix, tail = call(
        project, [(block, BF)] * 5, half, 3 * macs, 2 * small,
        pos, t2, near, w3, w_other,
    )
    prior = passed_along(tail, 1)
    (near,) = call(
        filtered_near, [(block, F32)], shifted, macs, small,
        pos, mix, reach, *both_taps,
    )
    conv, gated = call(
        filtered, [(block, F32), (block, BF)], shifted, macs, small // 2,
        pos, prior, near, q, reach, *both_taps,
    )
    (terms,) = call(
        out_terms, [((n_chips * CORE, part, LANES), BF)], [], 2 * macs, 2 * small,
        pos, gated, out_weight, ow_other,
    )
    later, _ = lax.optimization_barrier((pos, terms))
    own_near, own_far = call(turn, turned, [], macs, 4 * small, later, w3)
    block_out = summed(terms, ("x", "y", "core"))
    dgated, dconv, head = call(
        back_gate, [(block, F32), (block, BF), (block, BF)], whole, 2 * macs, small,
        pos, c0, out_weight, ow_other, q,
    )
    after = passed_along(head, -1)
    (near,) = call(back_near, [(block, F32)], shifted, macs, small, pos, dconv, rem, *both_taps)
    (dproj,) = call(
        back_filtered, [(triple, BF)], shifted, macs, small // 2,
        pos, after, near, k, v, dgated, conv, rem, *both_taps,
    )
    sides = [((Y * CORE, part, LANES), BF)]
    (far,) = call(grad_terms, sides, [], 3 * macs, 2 * small, pos, dproj, own_far, other_far)
    got = swapped(far, "x")
    (near,) = call(grad_terms, sides, [], 3 * macs, 2 * small, pos, dproj, own_near, other_near)
    return block_out, summed((f32(near) + f32(got)).astype(BF), ("y", "core"))


def solution(mesh):
    fine = Mesh(
        mesh.devices.reshape(mesh.shape["ctx"], X, Y, CORE), ("ctx", "x", "y", "core")
    )
    tp = ("x", "y", "core")
    placed = (P("ctx", tp), P("ctx", tp), P(None, None, tp), P(None, tp), P(tp, None), P())
    return jax.shard_map(
        block_step,
        mesh=fine,
        in_specs=placed,
        out_specs=(P("ctx", tp), P("ctx", tp)),
        check_vma=False,
    )
```
